32 devices in a mesh: win: 2 (over y), tile: 4 (over z), chan: 2 (over x), col: 2 (over core).
Axes of the slice: x: 2, y: 2, z: 4, core: 2. Of those that a mesh axis runs over, the one named last changes fastest.
Arguments:
- spectral_cube: float32 [2, 128, 128, 1024], P('chan', 'tile', 'win', 'col'), parts along dimension 2, may hold values from -32 to 32, as said below
- line_free: int32 [8, 256], P('win'), parts along dimension 0, may hold values from 0 to 1, as said below
- bad_flags: int32 [512], P('win'), parts along dimension 0, may hold values from 0 to 1, as said below
- kernel_widths: int32 [3], replicated, may hold values from 1 to 4
Outputs:
- significance: float32 [3, 256, 128, 1024], P(None, 'chan', ('win', 'tile'), 'col'), parts along dimension 2
The draws below stay inside these ranges and needn't reach their ends.
There are 2 independent parts, one for each index of `win`. The reference program is written for one: setup_inputs(seed, part) draws one part's arguments, and reference() takes and returns one part's arrays. A program takes and returns all parts, laid end to end along the dimension named above; an argument that names none is the same for every part. Nothing has to cross between parts.
Inputs may be any that keep to these rules, and one draw needn't show every extreme that they name: `spectral_cube`: brightness is a per-pixel cubic continuum plus channel noise. `line_free`: in each block of 16 rows the zeros form one run of 64 channels; in even-numbered blocks the run lies in the lower half of the channels, in odd-numbered blocks in the upper half. `bad_flags`: exactly 16 channels are flagged.
All inputs are finite; a program needn't handle non-finite values.
Results may differ from the reference program's by a relative error of at most 0.0003.
Values sent between devices are 32-bit elements; how exact they have to be, the bound alone decides.
No kernel may reach another device: no remote copies, remote signals or barrier semaphores. Data moves between devices by JAX's collectives and lax.ppermute only.
A program may use at most 64 MiB of HBM per device.

```python
import math
import jax
import jax.numpy as jnp
from jax import lax

C = 256
HALF = 8
REG = 16
KERNELS = 3
H = 64
W = 1024
CHG = 128
NREG = 4


def draw_spectral_cube(key, part):
    key_coeff, key_noise, key_scale = jax.random.split(key, 3)
    coords = 2.0 * jnp.arange(C).astype(jnp.float32) / (C - 1) - 1.0
    basis_all = jnp.stack([jnp.ones_like(coords), coords, 1.5 * coords * coords - 0.5, 2.5 * coords * coords * coords - 1.5 * coords])
    amplitudes = jnp.array([1.0, 0.5, 0.3, 0.2], jnp.float32)
    coeffs = jax.random.truncated_normal(key_coeff, -3.0, 3.0, (4, H, W), jnp.float32) * amplitudes[:, None, None]
    levels = jnp.exp(jax.random.uniform(key_scale, (C,), jnp.float32, math.log(0.5), math.log(2.0)))
    channel_noise = jax.random.truncated_normal(key_noise, -4.0, 4.0, (C, H, W), jnp.float32) * levels[:, None, None]
    continuum = jnp.einsum('ic,ihw->chw', basis_all, coeffs)
    return (continuum + channel_noise).reshape(C // CHG, CHG, H, W)


def draw_line_free(key, part):
    key_low, key_high = jax.random.split(jax.random.fold_in(key, 11), 2)
    starts_low = jax.random.randint(key_low, (NREG,), 0, C // 4 + 1)
    starts_high = jax.random.randint(key_high, (NREG,), C // 2, 3 * C // 4 + 1)
    parity = jnp.arange(NREG) % 2
    starts = jnp.where(parity == 0, starts_low, starts_high)
    channels = jnp.arange(C)[None, :]
    inside = (channels >= starts[:, None]) & (channels < starts[:, None] + C // 4)
    return jnp.where(inside, 0, 1).astype(jnp.int32)


def draw_bad_flags(key, part):
    order = jax.random.permutation(jax.random.fold_in(key, 23), C)
    return (order < C // 16).astype(jnp.int32)


def setup_inputs(seed: int = 0, part: int = 0) -> dict:
    seeds = jax.random.split(jax.random.key(seed), 5)
    part_splits = jax.random.split(jax.random.fold_in(seeds[4], part), 5)
    spectral_cube = draw_spectral_cube(jax.random.fold_in(jax.random.fold_in(seeds[4], part), 71), part)
    line_free = draw_line_free(jax.random.fold_in(jax.random.fold_in(seeds[4], part), 71), part)
    bad_flags = draw_bad_flags(jax.random.fold_in(jax.random.fold_in(seeds[4], part), 71), part)
    kernel_widths = jax.random.randint(seeds[3], (KERNELS,), 1, 5).astype(jnp.int32)
    return dict(spectral_cube=spectral_cube, line_free=line_free, bad_flags=bad_flags, kernel_widths=kernel_widths)


highest = lax.Precision.HIGHEST

def legendre(coords):
    return jnp.stack([jnp.ones_like(coords), coords, 1.5 * coords * coords - 0.5, 2.5 * coords * coords * coords - 1.5 * coords])

def channel_coords(indices, channel_total):
    return 2.0 * indices.astype(jnp.float32) / (channel_total - 1) - 1.0

def invert_small(matrices):
    dimension = matrices.shape[-1]
    identity = jnp.broadcast_to(jnp.eye(dimension, dtype=matrices.dtype), matrices.shape)
    augmented = jnp.concatenate([matrices, identity], axis=2)
    for pivot_at in range(dimension):
        pivot_row = augmented[:, pivot_at, :] / augmented[:, pivot_at, pivot_at:pivot_at + 1]
        updated = augmented - augmented[:, :, pivot_at:pivot_at + 1] * pivot_row[:, None, :]
        chosen = (jnp.arange(dimension) == pivot_at)[None, :, None]
        augmented = jnp.where(chosen, pivot_row[:, None, :], updated)
    return augmented[:, :, dimension:]

def gaussian_taps(kernel_widths):
    offsets = jnp.arange(-HALF, HALF + 1).astype(jnp.float32)
    sigmas = kernel_widths.astype(jnp.float32)
    unscaled = jnp.exp(-offsets[None, :] * offsets[None, :] / (2.0 * sigmas[:, None] * sigmas[:, None]))
    return unscaled / lax.optimization_barrier(jnp.sum(unscaled, axis=1, keepdims=True))

def median_three(edge_levels):
    below_level = edge_levels[:, :-2]
    middle = edge_levels[:, 1:-1]
    above_level = edge_levels[:, 2:]
    highest_one = jnp.maximum(jnp.maximum(below_level, middle), above_level)
    lowest_one = jnp.minimum(jnp.minimum(below_level, middle), above_level)
    return below_level + middle + above_level - highest_one - lowest_one

def reference(spectral_cube, line_free, bad_flags, kernel_widths):
    spectra = spectral_cube.reshape(C, H, W)
    basis_all = legendre(channel_coords(jnp.arange(C), C))
    good_mask = (1 - bad_flags).astype(jnp.float32)
    free_mask = line_free.astype(jnp.float32)
    weights = free_mask * good_mask[None, :]
    normal_matrix = jnp.einsum('rc,ic,jc->rij', weights, basis_all, basis_all, precision=highest)
    inverse = invert_small(normal_matrix)
    weight_rows = jnp.repeat(weights, REG, axis=0)
    moments = jnp.einsum('ic,chw->ihw', basis_all, spectra * weight_rows.T[:, :, None], precision=highest)
    inverse_rows = jnp.repeat(inverse, REG, axis=0)
    coeffs = jnp.einsum('hij,jhw->ihw', inverse_rows, moments, precision=highest)
    residual = spectra - jnp.einsum('ic,ihw->chw', basis_all, coeffs, precision=highest)
    kernel_taps = gaussian_taps(kernel_widths)
    padded = jnp.pad(residual, ((0, 0), (HALF, HALF), (HALF, HALF)))
    free_rows = jnp.repeat(free_mask, REG, axis=0).T

    def smooth_one(tap_row):
        across = tap_row[0] * padded[:, :, 0:W]
        for offset in range(1, 2 * HALF + 1):
            across = across + tap_row[offset] * padded[:, :, offset:offset + W]
        both_axes = tap_row[0] * across[:, 0:H, :]
        for offset in range(1, 2 * HALF + 1):
            both_axes = both_axes + tap_row[offset] * across[:, offset:offset + H, :]
        line_power = lax.optimization_barrier(jnp.sum(free_rows[:, :, None] * both_axes * both_axes, axis=(1, 2)))
        return (both_axes, line_power)
    smoothed, line_power = lax.map(smooth_one, kernel_taps)
    counts = REG * W * lax.optimization_barrier(jnp.sum(free_mask, axis=0))
    noise_level = jnp.sqrt(line_power / counts[None, :] + 1e-06)
    edge_levels = jnp.pad(noise_level, ((0, 0), (1, 1)))
    noise_floor = median_three(edge_levels)
    return smoothed * good_mask[None, :, None, None] / noise_floor[:, :, None, None]
```

```python
import functools

import jax
import jax.numpy as jnp
from jax import lax
from jax.experimental import pallas as pl
from jax.experimental.pallas import tpu as pltpu
from jax.sharding import PartitionSpec as P

HALF = 8
REG = 16
LANES = 128
SUB = 8
CHUNKS = (1, 1, 1, 1)


highest = lax.Precision.HIGHEST


def legendre(coords):
    return jnp.stack(
        [
            jnp.ones_like(coords),
            coords,
            1.5 * coords * coords - 0.5,
            2.5 * coords * coords * coords - 1.5 * coords,
        ]
    )


def channel_coords(indices, channel_total):
    return 2.0 * indices.astype(jnp.float32) / (channel_total - 1) - 1.0


def invert_small(matrices):
    dimension = matrices.shape[-1]
    identity = jnp.broadcast_to(jnp.eye(dimension, dtype=matrices.dtype), matrices.shape)
    augmented = jnp.concatenate([matrices, identity], axis=2)
    for pivot_at in range(dimension):
        pivot_row = augmented[:, pivot_at, :] / augmented[:, pivot_at, pivot_at : pivot_at + 1]
        updated = augmented - augmented[:, :, pivot_at : pivot_at + 1] * pivot_row[:, None, :]
        chosen = (jnp.arange(dimension) == pivot_at)[None, :, None]
        augmented = jnp.where(chosen, pivot_row[:, None, :], updated)
    return augmented[:, :, dimension:]


def gaussian_taps(kernel_widths):
    offsets = jnp.arange(-HALF, HALF + 1).astype(jnp.float32)
    sigmas = kernel_widths.astype(jnp.float32)
    unscaled = jnp.exp(
        -offsets[None, :] * offsets[None, :] / (2.0 * sigmas[:, None] * sigmas[:, None])
    )
    return unscaled / jnp.sum(unscaled, axis=1, keepdims=True)


def median_three(below_level, middle, above_level):
    highest_one = jnp.maximum(jnp.maximum(below_level, middle), above_level)
    lowest_one = jnp.minimum(jnp.minimum(below_level, middle), above_level)
    return below_level + middle + above_level - highest_one - lowest_one


def band(taps, offsets):
    total = jnp.zeros((taps.shape[0],) + offsets.shape, jnp.float32)
    for at in range(2 * HALF + 1):
        total = jnp.where(offsets == at, taps[:, at, None, None], total)
    return total


def split_two(values):
    high = lax.reduce_precision(values, 8, 7)
    return high.astype(jnp.bfloat16), (values - high).astype(jnp.bfloat16)


def pieces_of(refs, turns):
    own_ref, main_refs, low_ref, high_ref = refs
    rows = main_refs[0].shape[2] if main_refs else own_ref.shape[2] - 2 * HALF

    def piece(k, c, g):
        if k == 0:
            return own_ref[0, c, SUB * g : SUB * g + SUB, :]
        if g == 0:
            return low_ref[0, k - 1, c, :, :]
        if g == rows // SUB + 1:
            return high_ref[0, k - 1, c, :, :]
        return main_refs[k - 1][0, c, SUB * (g - 1) : SUB * g, :]

    return piece


def moments_kernel(turns, groups, per_turn, step_channels, *refs):
    weight_ref, basis_ref, own_ref = refs[:3]
    main_refs = refs[3 : 3 + turns - 1]
    low_ref, high_ref, out_ref = refs[3 + turns - 1 :]
    piece = pieces_of((own_ref, main_refs, low_ref, high_ref), turns)
    step = pl.program_id(1)

    @pl.when(step == 0)
    def _():
        out_ref[...] = jnp.zeros_like(out_ref)

    for g in range(groups):
        rows = slice(SUB * g, SUB * g + SUB)
        sums = [out_ref[0, i, rows, :] for i in range(4)]
        for k in range(turns):
            for c in range(step_channels):
                channel = k * per_turn + step * step_channels + c
                weighted = piece(k, c, g) * weight_ref[g, channel]
                sums[0] = sums[0] + weighted
                for i in range(1, 4):
                    sums[i] = sums[i] + weighted * basis_ref[i, channel]
        for i in range(4):
            out_ref[0, i, rows, :] = sums[i]


def rows_kernel(turns, groups, per_turn, step_channels, out_rows, *refs):
    inverse_ref, basis_ref, band_ref, mine_ref, other_ref, own_ref = refs[:6]
    main_refs = refs[6 : 6 + turns - 1]
    low_ref, high_ref, out_ref = refs[6 + turns - 1 :]
    piece = pieces_of((own_ref, main_refs, low_ref, high_ref), turns)
    step = pl.program_id(1)
    coeffs = []
    for g in range(groups):
        rows = slice(SUB * g, SUB * g + SUB)
        totals = [mine_ref[0, j, rows, :] + other_ref[0, j, rows, :] for j in range(4)]
        coeffs.append(
            [
                sum(inverse_ref[g, 4 * i + j] * totals[j] for j in range(4))
                for i in range(4)
            ]
        )
    rows_band = band_ref[...]
    kernels = rows_band.shape[0] // out_rows
    for k in range(turns):
        columns = []
        for c in range(step_channels):
            channel = k * per_turn + step * step_channels + c
            parts = []
            for g in range(groups):
                fit = coeffs[g][0]
                for i in range(1, 4):
                    fit = fit + coeffs[g][i] * basis_ref[i, channel]
                parts.append(piece(k, c, g) - fit)
            columns.append(jnp.concatenate(parts, axis=0))
        residual = jnp.concatenate(columns, axis=1)
        high = residual.astype(jnp.bfloat16)
        low = (residual - high.astype(jnp.float32)).astype(jnp.bfloat16)
        stacked = jnp.concatenate([high, low, high], axis=0)
        smoothed = jnp.dot(rows_band, stacked, preferred_element_type=jnp.float32)
        for c in range(step_channels):
            for q in range(kernels):
                out_ref[0, q, k, c, :, :] = smoothed[
                    q * out_rows : (q + 1) * out_rows, c * LANES : (c + 1) * LANES
                ]


def columns_kernel(far_edge, *refs):
    if far_edge:
        side_ref, wide_ref, here_ref, near_ref, out_ref, power_ref = refs
    else:
        side_ref, wide_ref, here_ref, near_ref, far_ref, out_ref, power_ref = refs
    channels, rows = here_ref.shape[3], here_ref.shape[4]
    flat = (channels * rows, LANES)
    here = here_ref[0, 0, 0].reshape(flat)
    near = near_ref[0, 0, 0].reshape(flat)
    lane = lax.broadcasted_iota(jnp.int32, (1, LANES), 1)
    lane = jnp.where(side_ref[0] == 1, lane, LANES - 1 - lane)
    far = jnp.zeros_like(near) if far_edge else far_ref[0, 0, 0].reshape(flat)
    edges = jnp.where(lane >= LANES // 2, near, far)
    wide = wide_ref[0]
    both = jnp.concatenate([here, edges], axis=1)
    high = both.astype(jnp.bfloat16)
    low = (both - high.astype(jnp.float32)).astype(jnp.bfloat16)
    first = jnp.dot(high, wide, preferred_element_type=jnp.float32)
    second = jnp.dot(low, wide[:, :LANES], preferred_element_type=jnp.float32)
    result = first[:, :LANES] + (first[:, LANES:] + second)
    shaped = result.reshape(channels, rows, LANES)
    out_ref[0, 0] = shaped
    power_ref[0, 0] = jnp.sum(shaped * shaped, axis=1)


def scale_kernel(tiles, order_ref, side_ref, scale_ref, *refs):
    out_ref = refs[tiles]
    scale = scale_ref[0, 0][:, None, :]

    def write(places):
        for p, place in enumerate(places):
            out_ref[0, :, :, place * LANES : (place + 1) * LANES] = refs[p][0, 0] * scale

    @pl.when(side_ref[0] == 1)
    def _():
        write(range(tiles))

    @pl.when(side_ref[0] == 0)
    def _():
        write(range(tiles - 1, -1, -1))


def smem():
    return pl.BlockSpec(memory_space=pltpu.SMEM)


def params(limit_mib, axes):
    return pltpu.CompilerParams(
        dimension_semantics=("arbitrary",) * axes, vmem_limit_bytes=limit_mib << 20
    )


def swap(values, axis):
    return lax.ppermute(values, axis, [(0, 1), (1, 0)])


def sum_over(values, axis):
    size = lax.axis_size(axis)
    if size & (size - 1):
        return lax.psum(values, axis)
    step = 1
    while step < size:
        values = values + lax.ppermute(values, axis, [(i, i ^ step) for i in range(size)])
        step *= 2
    return values


def body(spectral_cube, line_free, bad_flags, kernel_widths):
    turns = lax.axis_size("tile")
    tile_at = lax.axis_index("tile")
    chan_at = lax.axis_index("chan")
    chan_count = lax.axis_size("chan")
    side = lax.axis_index("col")
    assert lax.axis_size("col") == 2
    cube = spectral_cube[0]
    per_turn, full_rows, local_cols = cube.shape
    group_size = per_turn * turns
    local_rows = full_rows // turns
    window = local_rows + 2 * HALF
    groups = window // SUB
    tiles = local_cols // LANES
    assert local_rows == REG
    channel_total = line_free.shape[1]
    kernels = kernel_widths.shape[0]
    step_channels = max(1, 32 // turns)
    while per_turn % step_channels:
        step_channels -= 1
    steps = per_turn // step_channels
    f32 = jnp.float32

    good_mask = (1 - bad_flags).astype(f32)
    free_mask = line_free.astype(f32)
    weights = free_mask * good_mask[None, :]
    basis_all = legendre(channel_coords(jnp.arange(channel_total), channel_total))
    normal_matrix = jnp.einsum("rc,ic,jc->rij", weights, basis_all, basis_all, precision=highest)
    inverse_all = invert_small(normal_matrix)
    group_first = chan_at * group_size
    row_first = tile_at * local_rows

    def turned(values):
        lead = values.shape[0]
        mine = lax.dynamic_slice_in_dim(values, group_first, group_size, 1)
        mine = mine.reshape(lead, turns, per_turn)[:, ::-1]
        twice = jnp.concatenate([mine, mine], axis=1)
        start = (turns - 1 - tile_at) % turns
        return lax.dynamic_slice_in_dim(twice, start, turns, 1).reshape(lead, group_size)

    group_rows = row_first - HALF + SUB * jnp.arange(groups)
    group_region = jnp.clip(group_rows // REG, 0, line_free.shape[0] - 1)
    pick = (group_region[:, None] == jnp.arange(line_free.shape[0])[None, :]).astype(f32)
    inverse_groups = jnp.einsum(
        "gr,rm->gm", pick, inverse_all.reshape(-1, 16), precision=highest
    )
    turned_basis = turned(basis_all)
    turned_weights = turned(jnp.einsum("gr,rc->gc", pick, weights, precision=highest))

    taps = gaussian_taps(kernel_widths)
    row_offsets = jnp.arange(window)[None, :] - jnp.arange(local_rows)[:, None]
    rows_high, rows_low = split_two(band(taps, row_offsets).reshape(-1, window))
    row_band = jnp.concatenate([rows_high, rows_high, rows_low], axis=1)
    lane_in = jnp.arange(LANES)
    lane_edge = jnp.where(lane_in >= LANES // 2, lane_in - LANES, lane_in + LANES)
    positions = jnp.concatenate([lane_in, lane_edge])
    column_offsets = positions[:, None] - lane_in[None, :] + HALF
    column_band = jnp.concatenate(split_two(band(taps, column_offsets)), axis=2)

    def place(p):
        return jnp.where(side == 1, p, tiles - 1 - p) * LANES

    up = [(i, i + 1) for i in range(turns - 1)]
    down = [(i + 1, i) for i in range(turns - 1)]
    padded = jnp.pad(cube, ((0, 0), (HALF, HALF), (0, 0)))
    plain = jnp.asarray(side, jnp.int32).reshape(1)

    chunk_tiles = list(CHUNKS) if sum(CHUNKS) == tiles else [1] * tiles
    firsts = [sum(chunk_tiles[:j]) for j in range(len(chunk_tiles))]
    mains = []
    owns = []
    for first, count in zip(firsts, chunk_tiles):
        received = []
        for k in range(turns):
            target = ((tile_at + k) % turns) * local_rows
            rows, source = (window, padded) if k == 0 else (local_rows, cube)
            sent = jnp.stack(
                [
                    lax.dynamic_slice(
                        source, (0, target, place(first + t)), (per_turn, rows, LANES)
                    )
                    for t in range(count)
                ]
            )
            if k:
                sent = lax.ppermute(sent, "tile", [(i, (i + k) % turns) for i in range(turns)])
                received.append(sent)
            else:
                owns.append(sent)
        mains.append(received)

    smooth_rows = []
    for received, own, count in zip(mains, owns, chunk_tiles):
        blocks = [own[:, :, HALF : HALF + local_rows]] + received
        low = high = jnp.zeros((count, 1, per_turn, HALF, LANES), f32)
        if turns > 1:
            low = lax.ppermute(
                jnp.stack([b[:, :, local_rows - HALF :] for b in blocks[: turns - 1]], axis=1),
                "tile",
                up,
            )
            high = lax.ppermute(
                jnp.stack([b[:, :, :HALF] for b in blocks[2:] + blocks[:1]], axis=1),
                "tile",
                down,
            )
        pieces = [own] + received + [low, high]
        piece_specs = (
            [pl.BlockSpec((1, step_channels, window, LANES), lambda j, s: (j, s, 0, 0))]
            + [pl.BlockSpec((1, step_channels, local_rows, LANES), lambda j, s: (j, s, 0, 0))]
            * (turns - 1)
            + [
                pl.BlockSpec(
                    (1, low.shape[1], step_channels, HALF, LANES), lambda j, s: (j, 0, s, 0, 0)
                )
            ]
            * 2
        )
        moment_spec = pl.BlockSpec((1, 4, window, LANES), lambda j, s: (j, 0, 0, 0))
        volume = count * group_size * window * LANES
        mine = pl.pallas_call(
            functools.partial(moments_kernel, turns, groups, per_turn, step_channels),
            grid=(count, steps),
            in_specs=[smem(), smem()] + piece_specs,
            out_specs=moment_spec,
            out_shape=jax.ShapeDtypeStruct((count, 4, window, LANES), f32),
            compiler_params=params(16, 2),
            cost_estimate=pl.CostEstimate(
                flops=8 * volume, bytes_accessed=4 * volume, transcendentals=0
            ),
            name="moments",
        )(turned_weights, turned_basis, *pieces)
        if chan_count == 2:
            other = swap(mine, "chan")
        else:
            other = lax.psum(mine, "chan") - mine
        smooth_rows.append(
            pl.pallas_call(
                functools.partial(
                    rows_kernel, turns, groups, per_turn, step_channels, local_rows
                ),
                grid=(count, steps),
                in_specs=[
                    smem(),
                    smem(),
                    pl.BlockSpec(row_band.shape, lambda j, s: (0, 0)),
                    moment_spec,
                    moment_spec,
                ]
                + piece_specs,
                out_specs=pl.BlockSpec(
                    (1, kernels, turns, step_channels, local_rows, LANES),
                    lambda j, s: (j, 0, 0, s, 0, 0),
                ),
                out_shape=jax.ShapeDtypeStruct(
                    (count, kernels, turns, per_turn, local_rows, LANES), f32
                ),
                compiler_params=params(24, 2),
                cost_estimate=pl.CostEstimate(
                    flops=200 * volume, bytes_accessed=10 * volume, transcendentals=0
                ),
                name="rows",
            )(inverse_groups, turned_basis, row_band, mine, other, *pieces)
        )

    halo = swap(smooth_rows[0][:1], "col")

    def tile_of(p):
        for rows, first, count in zip(smooth_rows, firsts, chunk_tiles):
            if first <= p < first + count:
                return rows, p - first

    tile_block = (1, 1, 1, per_turn, local_rows, LANES)
    results = []
    powers = []
    for p in range(tiles):
        sources = [tile_of(p), (halo, 0) if p == 0 else tile_of(p - 1)]
        far_edge = p == tiles - 1
        if not far_edge:
            sources.append(tile_of(p + 1))
        volume = kernels * group_size * local_rows * LANES
        result, power = pl.pallas_call(
            functools.partial(columns_kernel, far_edge),
            grid=(kernels, turns),
            in_specs=[smem(), pl.BlockSpec((1, 2 * LANES, 2 * LANES), lambda q, k: (q, 0, 0))]
            + [
                pl.BlockSpec(tile_block, functools.partial(lambda at, q, k: (at, q, k, 0, 0, 0), at))
                for _, at in sources
            ],
            out_specs=[
                pl.BlockSpec((1, 1, per_turn, local_rows, LANES), lambda q, k: (q, k, 0, 0, 0)),
                pl.BlockSpec((1, 1, per_turn, LANES), lambda q, k: (q, k, 0, 0)),
            ],
            out_shape=[
                jax.ShapeDtypeStruct((kernels, turns, per_turn, local_rows, LANES), f32),
                jax.ShapeDtypeStruct((kernels, turns, per_turn, LANES), f32),
            ],
            compiler_params=params(24, 2),
            cost_estimate=pl.CostEstimate(
                flops=1500 * volume, bytes_accessed=16 * volume, transcendentals=0
            ),
            name="columns",
        )(plain, column_band, *[rows for rows, _ in sources])
        results.append(result)
        powers.append(power)

    power = jnp.sum(sum(powers), axis=3)
    power = power[:, ::-1]
    power = jnp.concatenate([power, power], axis=1)
    power = lax.dynamic_slice_in_dim(power, (turns - 1 - tile_at) % turns, turns, 1)
    power = power.reshape(kernels, group_size)
    block_free = lax.dynamic_slice(
        jnp.repeat(free_mask, REG, axis=0), (row_first, group_first), (local_rows, group_size)
    )
    power = power * block_free[0]
    power = sum_over(sum_over(power, "col"), "tile")
    counts_all = REG * local_cols * lax.axis_size("col") * jnp.sum(free_mask, axis=0)
    counts = lax.dynamic_slice_in_dim(counts_all, group_first, group_size, 0)
    level = jnp.sqrt(power / counts[None, :] + 1e-06)
    first_level, last_level = level[:, :1], level[:, -1:]
    if chan_count == 2:
        met = swap(jnp.where(chan_at == 0, last_level, first_level), "chan")
        before = jnp.where(chan_at == 1, met, 0.0)
        after = jnp.where(chan_at == 0, met, 0.0)
    else:
        before = lax.ppermute(last_level, "chan", [(i, i + 1) for i in range(chan_count - 1)])
        after = lax.ppermute(first_level, "chan", [(i + 1, i) for i in range(chan_count - 1)])
    edged = jnp.concatenate([before, level, after], axis=1)
    floor = median_three(edged[:, :-2], edged[:, 1:-1], edged[:, 2:])
    good_group = lax.dynamic_slice_in_dim(good_mask, group_first, group_size, 0)
    scale = (good_group[None, :] / floor).reshape(kernels, turns, per_turn, 1)
    scale = jnp.broadcast_to(scale, (kernels, turns, per_turn, LANES))

    order = ((tile_at - jnp.arange(turns)) % turns).astype(jnp.int32)
    volume = kernels * group_size * local_rows * local_cols
    return pl.pallas_call(
        functools.partial(scale_kernel, tiles),
        grid_spec=pltpu.PrefetchScalarGridSpec(
            num_scalar_prefetch=2,
            grid=(kernels, turns),
            in_specs=[pl.BlockSpec((1, 1, per_turn, LANES), lambda q, k, o, s: (q, o[k], 0, 0))]
            + [
                pl.BlockSpec(
                    (1, 1, per_turn, local_rows, LANES), lambda q, k, o, s: (q, k, 0, 0, 0)
                )
            ]
            * tiles,
            out_specs=pl.BlockSpec(
                (1, per_turn, local_rows, local_cols), lambda q, k, o, s: (q, o[k], 0, 0)
            ),
        ),
        out_shape=jax.ShapeDtypeStruct((kernels, group_size, local_rows, local_cols), f32),
        compiler_params=params(16, 2),
        cost_estimate=pl.CostEstimate(
            flops=volume, bytes_accessed=8 * volume, transcendentals=0
        ),
        name="scale",
    )(order, plain, scale, *results)


def solution(mesh):
    return jax.shard_map(
        body,
        mesh=mesh,
        in_specs=(P("chan", "tile", "win", "col"), P("win", None), P("win"), P()),
        out_specs=P(None, "chan", ("win", "tile"), "col"),
        check_vma=False,
    )
```
